32 devices in a mesh: dp: 8 (over z, y), expert: 4 (over x, core).
Axes of the slice: x: 2, y: 2, z: 4, core: 2. Of those that a mesh axis runs over, the one named last changes fastest.
Arguments:
- tokens: bfloat16 [4096, 2048], P(('dp', 'expert')), may hold values from -6 to 6
- expert_ids: int32 [4096, 1], P(('dp', 'expert')), may hold values from 0 to 1
- copy_choice: int32 [4096, 1], P(('dp', 'expert')), may hold values from 0 to 1
- gate_weights: float32 [4096, 1], P(('dp', 'expert')), may hold values from 0.05 to 1
- w_gate: bfloat16 [2048, 3072], P(None, 'expert'), may hold values from -0.125 to 0.125
- w_up: bfloat16 [2048, 3072], P(None, 'expert'), may hold values from -0.125 to 0.125
- w_down: bfloat16 [3072, 2048], P('expert'), may hold values from -0.15625 to 0.15625
Outputs:
- moe_out: bfloat16 [4096, 2048], P(('dp', 'expert'))
- expert_load: float32 [2], replicated
The draws below stay inside these ranges and needn't reach their ends.
Inputs may be any that keep to these rules, and one draw needn't show every extreme that they name: `expert_ids`: the 1 expert of a token are distinct.
All inputs are finite; a program needn't handle non-finite values.
Results may differ from the reference program's by a relative error of at most 0.0049.
Values may be sent and summed in bfloat16 or wider, within the bound.
No kernel may reach another device: no remote copies, remote signals or barrier semaphores. Data moves between devices by JAX's collectives and lax.ppermute only.
A program may use at most 64 MiB of HBM per device.

```python
import math
import jax
import jax.numpy as jnp
from jax import lax

D = 2048
FF = 1536
TOK_DEV = 128
EXPERTS = 2
TOPK = 1
CAP = 32
TOKENS = 4096
N_DP = 8
N_EXPERT = 4


def touch_ends(array, key, smallest, top_value):
    longest = array.shape.index(max(array.shape))
    spots = []
    for shift in (0, 1):
        where = [jax.random.randint(jax.random.fold_in(key, axis), (), 0, length) for axis, length in enumerate(array.shape)]
        where[longest] = (where[longest] + shift) % array.shape[longest]
        spots.append(tuple(where))
    return array.at[spots[0]].set(smallest).at[spots[1]].set(top_value)


def levels(rng, shape, cuts, low, top_value):
    gain, own = 1.0, jax.random.fold_in(rng, 6)
    for dim, blocks in cuts:
        heights = jnp.exp(jax.random.uniform(jax.random.fold_in(own, dim), (blocks,), jnp.float32, low / len(cuts), top_value / len(cuts)))
        gain = gain * jnp.repeat(heights, shape[dim] // blocks).reshape([-1 if axis == dim else 1 for axis in range(len(shape))])
    return gain


def picks_of(stream_key, rows, count, top, lift):
    order = jax.random.permutation(jax.random.fold_in(stream_key, 1), count)
    favour = order
    for power in range(3):
        favour = favour * favour // count
    favour = favour * lift // count
    chance = jax.random.randint(jax.random.fold_in(stream_key, 2), (rows, count), 0, 4096) + favour
    fixed_rows = jax.random.permutation(jax.random.fold_in(stream_key, 3), rows)[jnp.arange(count) % rows]
    chance = jnp.where(jnp.arange(rows)[:, None] == fixed_rows[None, :], 1 << 14, chance)
    score = chance * count + jnp.arange(count)
    return lax.top_k(score.astype(jnp.int32), top)[1].astype(jnp.int32)


def noise(rng, dims, spread, limit, cuts=(), held_as=jnp.bfloat16):
    loudness = levels(rng, dims, cuts, -0.22, 0.18) if cuts else 1.0
    result = jax.random.normal(rng, dims, jnp.float32) * spread * loudness
    return jnp.minimum(jnp.maximum(result, -limit), limit).astype(held_as)


def setup_inputs(seed: int = 0) -> dict:
    arg_keys = jax.random.split(jax.random.key(seed), 8)
    tokens = noise(arg_keys[0], (TOKENS, D), 1.0, 6.0, ((0, 32),))
    expert_ids = picks_of(arg_keys[1], TOKENS, EXPERTS, TOPK, 8192)
    copy_choice = touch_ends(jax.random.randint(arg_keys[2], (TOKENS, TOPK), 0, 2), jax.random.fold_in(arg_keys[2], 1), 0, 1).astype(jnp.int32)
    gate_weights = jnp.clip(jnp.exp(math.log(1.0) - 2.9957323 * jax.random.uniform(arg_keys[3], (TOKENS, TOPK), jnp.float32) ** levels(arg_keys[3], (TOKENS, TOPK), ((0, 32),), -0.2, 0.2)), 0.05, 1.0)
    w_gate = noise(arg_keys[4], (D, EXPERTS * FF), D ** -0.5, 0.125, ((1, 4),))
    w_up = noise(arg_keys[5], (D, EXPERTS * FF), D ** -0.5, 0.125, ((1, 4),))
    w_down = noise(arg_keys[6], (EXPERTS * FF, D), FF ** -0.5, 0.15625, ((0, 4),))
    return {"tokens": tokens, "expert_ids": expert_ids, "copy_choice": copy_choice, "gate_weights": gate_weights, "w_gate": w_gate, "w_up": w_up, "w_down": w_down}


def expert_pass(inputs, weight_gate, weight_up, weight_down):
    gate_act = jnp.dot(inputs, weight_gate, preferred_element_type=jnp.float32)
    up_act = jnp.dot(inputs, weight_up, preferred_element_type=jnp.float32)
    hidden = (jax.nn.silu(gate_act) * up_act).astype(jnp.bfloat16)
    return jnp.dot(hidden, weight_down, preferred_element_type=jnp.float32)


def reference(tokens, expert_ids, copy_choice, gate_weights, w_gate, w_up, w_down):
    devices = N_DP * N_EXPERT
    per_block = TOK_DEV * TOPK
    route_keys = (expert_ids * 2 + copy_choice).reshape(devices, per_block)
    onehot = (route_keys[:, :, None] == jnp.arange(2 * EXPERTS, dtype=jnp.int32)[None, None, :]).astype(jnp.int32)
    before = jnp.cumsum(onehot, axis=1) - onehot
    slot_rank = jnp.sum(before * onehot, axis=2)
    retained = slot_rank < CAP
    weighted = jnp.where(retained.reshape(TOKENS, TOPK), gate_weights, jnp.zeros_like(gate_weights))

    block_ids = jnp.arange(devices, dtype=jnp.int32)[:, None]
    route_pos = jnp.arange(per_block, dtype=jnp.int32)[None, :]
    token_index = block_ids * TOK_DEV + route_pos // TOPK
    flat_route = block_ids * per_block + route_pos
    place = jnp.where(retained, route_keys * CAP + slot_rank, 2 * EXPERTS * CAP)
    slot_count = 2 * EXPERTS * CAP + 1
    slot_token = jnp.full((devices, slot_count), -1, jnp.int32)
    slot_token = slot_token.at[block_ids, place].set(token_index)
    slot_route = jnp.full((devices, slot_count), -1, jnp.int32)
    slot_route = slot_route.at[block_ids, place].set(flat_route)
    slot_token = slot_token[:, :-1].reshape(devices, EXPERTS, 2 * CAP)
    slot_route = slot_route[:, :-1].reshape(devices, EXPERTS, 2 * CAP)
    flat_gate = weighted.reshape(-1)

    def one_expert(running, expert_id):
        start = (expert_id * FF).astype(jnp.int32)
        weight_gate = lax.dynamic_slice_in_dim(w_gate, start, FF, 1)
        weight_up = lax.dynamic_slice_in_dim(w_up, start, FF, 1)
        weight_down = lax.dynamic_slice_in_dim(w_down, start, FF, 0)
        rows_tok = lax.dynamic_index_in_dim(slot_token, expert_id, 1, keepdims=False).reshape(-1)
        rows_route = lax.dynamic_index_in_dim(slot_route, expert_id, 1, keepdims=False).reshape(-1)
        valid = rows_tok >= 0
        safe_tok = jnp.where(valid, rows_tok, 0)
        safe_route = jnp.where(valid, rows_route, 0)
        inputs = jnp.where(valid[:, None], tokens[safe_tok], jnp.zeros((), tokens.dtype))
        share = jnp.where(valid, flat_gate[safe_route], jnp.zeros((), jnp.float32))
        expert_out = expert_pass(inputs, weight_gate, weight_up, weight_down)
        running = running.at[safe_tok].add(share[:, None] * expert_out)
        load = jnp.sum(jnp.where(expert_ids == expert_id, weighted, jnp.zeros_like(weighted)))
        return running, load

    initial = jnp.zeros((TOKENS, D), jnp.float32)
    summed, load_list = lax.scan(one_expert, initial, jnp.arange(EXPERTS, dtype=jnp.int32))
    return summed.astype(jnp.bfloat16), load_list / TOKENS
```

```python
import jax
import jax.numpy as jnp
from jax import lax
from jax.sharding import PartitionSpec as P


def swap(value, axis, mask):
    pairs = [(source, source ^ mask) for source in range(lax.axis_size(axis))]
    return lax.ppermute(value, axis, pairs)


def shift(value, step):
    members = lax.axis_size("expert")
    pairs = [(source, (source + 2 * step) % members) for source in range(members)]
    return lax.ppermute(value, "expert", pairs)


def tree_sum(value, axis):
    terms = [value] + [swap(value, axis, mask) for mask in range(1, lax.axis_size(axis))]
    while len(terms) > 1:
        terms = [terms[i] + terms[i + 1] for i in range(0, len(terms), 2)]
    return terms[0]


def expert_pass(inputs, weight_gate, weight_up, weight_down):
    gate_act = jnp.dot(inputs, weight_gate, preferred_element_type=jnp.float32)
    up_act = jnp.dot(inputs, weight_up, preferred_element_type=jnp.float32)
    hidden = (jax.nn.silu(gate_act) * up_act).astype(jnp.bfloat16)
    return jnp.dot(hidden, weight_down, preferred_element_type=jnp.float32)


def local(tokens, expert_ids, copy_choice, gate_weights, w_gate, w_up, w_down):
    members = lax.axis_size("expert")
    experts = members // 2
    tok_rows, chosen = expert_ids.shape
    features = tokens.shape[1]
    capacity = max(2, tok_rows * chosen // (2 * experts))
    rows = 2 * capacity
    sections = 2 * experts
    own_expert = lax.axis_index("expert") // 2
    relative = expert_ids - own_expert
    relative = jnp.where(relative < 0, relative + experts, relative)
    route_keys = (relative * 2 + copy_choice).reshape(-1)
    onehot = (route_keys[:, None] == jnp.arange(sections, dtype=jnp.int32)[None, :]).astype(
        jnp.int32
    )
    before = jnp.cumsum(onehot, axis=0) - onehot
    slot_rank = jnp.sum(before * onehot, axis=1)
    retained = slot_rank < capacity
    target = jnp.where(retained, route_keys * capacity + slot_rank, -1).reshape(tok_rows, chosen)
    places = jnp.arange(sections * capacity, dtype=jnp.int32)
    matches = places[:, None, None] == target[None, :, :]
    dispatch = jnp.any(matches, axis=2).astype(jnp.bfloat16)
    packed = jnp.dot(dispatch, tokens, preferred_element_type=jnp.float32).astype(jnp.bfloat16)
    packed = packed.reshape(experts, rows, features)

    arrived = [shift(packed[step], step) for step in range(1, experts)]
    kept_gate = jnp.where(retained.reshape(tok_rows, chosen), gate_weights, 0.0)
    expert_match = expert_ids[:, :, None] == jnp.arange(experts, dtype=jnp.int32)[None, None, :]
    local_load = jnp.sum(jnp.where(expert_match, kept_gate[:, :, None], 0.0), axis=(0, 1))
    load_sum = tree_sum(tree_sum(local_load, "expert"), "dp")
    expert_load = load_sum / (tok_rows * lax.axis_size("dp") * members)

    def serve(mine):
        count = mine.shape[0]
        both = jnp.concatenate([mine, swap(mine, "expert", 1)], axis=0)
        partial = expert_pass(both, w_gate, w_up, w_down)
        other = swap(partial[count:].astype(jnp.bfloat16), "expert", 1)
        return (partial[:count] + other.astype(jnp.float32)).astype(jnp.bfloat16)

    near = serve(packed[0])
    far = serve(jnp.concatenate(arrived, axis=0))
    returned = [shift(far[(step - 1) * rows : step * rows], -step) for step in range(1, experts)]
    outputs = jnp.concatenate([near] + returned, axis=0)
    combined = jnp.zeros((tok_rows, features), jnp.float32)
    for choice in range(chosen):
        select = (target[:, choice : choice + 1] == places[None, :]).astype(jnp.bfloat16)
        chosen_rows = jnp.dot(select, outputs, preferred_element_type=jnp.float32)
        combined = combined + gate_weights[:, choice : choice + 1] * chosen_rows
    return (combined.astype(jnp.bfloat16), expert_load)


def solution(mesh):
    return jax.shard_map(
        local,
        mesh=mesh,
        in_specs=(
            P(("dp", "expert"), None),
            P(("dp", "expert"), None),
            P(("dp", "expert"), None),
            P(("dp", "expert"), None),
            P(None, "expert"),
            P(None, "expert"),
            P("expert", None),
        ),
        out_specs=(P(("dp", "expert"), None), P()),
        check_vma=False,
    )
```

```python
import functools

import jax
import jax.numpy as jnp
from jax import lax
from jax.experimental import pallas as pl
from jax.experimental.pallas import tpu as pltpu
from jax.sharding import PartitionSpec as P

VMEM = pl.BlockSpec(memory_space=pltpu.VMEM)


def swap(value, axis, mask):
    pairs = [(source, source ^ mask) for source in range(lax.axis_size(axis))]
    return lax.ppermute(value, axis, pairs)


def shift(value, step):
    members = lax.axis_size("expert")
    pairs = [(source, (source + 2 * step) % members) for source in range(members)]
    return lax.ppermute(value, "expert", pairs)


def pack_kernel(experts, capacity, ids_ref, copy_ref, gate_ref, tokens_ref, target_ref, load_ref, *packed_refs):
    chosen, tok_rows = ids_ref.shape
    rows = 2 * capacity
    sections = 2 * experts
    own = lax.axis_index("expert") // 2
    section = lax.broadcasted_iota(jnp.int32, (max(16, sections), tok_rows), 0)
    keys, hots = [], []
    for k in range(chosen):
        relative = ids_ref[k : k + 1, :] - own
        relative = jnp.where(relative < 0, relative + experts, relative)
        keys.append(relative * 2 + copy_ref[k : k + 1, :])
        hots.append(jnp.where(section == keys[k], 1.0, 0.0))
    total = functools.reduce(lambda a, b: a + b, hots)
    earlier = lax.broadcasted_iota(jnp.int32, (tok_rows, tok_rows), 0) < lax.broadcasted_iota(
        jnp.int32, (tok_rows, tok_rows), 1
    )
    before = jnp.dot(
        total.astype(jnp.bfloat16),
        jnp.where(earlier, 1.0, 0.0).astype(jnp.bfloat16),
        preferred_element_type=jnp.float32,
    )
    targets = []
    served = lax.broadcasted_iota(jnp.int32, (load_ref.shape[0], tok_rows), 0)
    load = jnp.zeros((load_ref.shape[0], tok_rows), jnp.float32)
    for k in range(chosen):
        rank = jnp.sum(before * hots[k], axis=0, keepdims=True).astype(jnp.int32)
        before = before + hots[k]
        retained = rank < capacity
        target = jnp.where(retained, keys[k] * capacity + rank, -1)
        targets.append(target)
        target_ref[k : k + 1, :] = target
        kept = jnp.where(retained, gate_ref[k : k + 1, :], 0.0)
        load = load + jnp.where(served == ids_ref[k : k + 1, :], kept, 0.0)
    load_ref[...] = jnp.broadcast_to(jnp.sum(load, axis=1, keepdims=True), load_ref.shape)
    tokens = tokens_ref[...]
    place = lax.broadcasted_iota(jnp.int32, (rows, tok_rows), 0)
    for step in list(range(1, experts)) + [0]:
        match = functools.reduce(
            lambda a, b: a | b, [place + step * rows == target for target in targets]
        )
        packed = jnp.dot(
            jnp.where(match, 1.0, 0.0).astype(jnp.bfloat16), tokens, preferred_element_type=jnp.float32
        )
        packed_refs[step][...] = packed.astype(jnp.bfloat16)


def expert_kernel(mine_ref, other_ref, gate_ref, up_ref, down_ref, part_ref, send_ref):
    count = mine_ref.shape[0]
    both = jnp.concatenate([mine_ref[...], other_ref[...]], axis=0)
    gate_act = jnp.dot(both, gate_ref[...], preferred_element_type=jnp.float32)
    up_act = jnp.dot(both, up_ref[...], preferred_element_type=jnp.float32)
    hidden = (gate_act / (1.0 + jnp.exp(-gate_act)) * up_act).astype(jnp.bfloat16)
    out = jnp.dot(hidden, down_ref[...], preferred_element_type=jnp.float32)
    part_ref[...] = out[:count]
    send_ref[...] = out[count:].astype(jnp.bfloat16)


def merge_kernel(part_ref, other_ref, out_ref):
    out_ref[...] = (part_ref[...] + other_ref[...].astype(jnp.float32)).astype(jnp.bfloat16)


def combine_kernel(target_ref, gate_ref, *refs):
    result_refs, out_ref = refs[:-1], refs[-1]
    chosen, tok_rows = target_ref.shape
    results = jnp.concatenate([ref[...] for ref in result_refs], axis=0)
    slots = results.shape[0]
    slot = lax.broadcasted_iota(jnp.int32, (tok_rows, slots), 1)
    combined = None
    for k in range(chosen):
        column = jnp.broadcast_to(target_ref[k : k + 1, :], (slots, tok_rows)).T
        scale = jnp.broadcast_to(gate_ref[k : k + 1, :], (128, tok_rows)).T[:, :1]
        select = jnp.where(column == slot, 1.0, 0.0).astype(jnp.bfloat16)
        term = scale * jnp.dot(select, results, preferred_element_type=jnp.float32)
        combined = term if combined is None else combined + term
    out_ref[...] = combined.astype(jnp.bfloat16)


def call(kernel, outs, count, name, megabytes):
    return pl.pallas_call(
        kernel,
        out_shape=outs,
        in_specs=[VMEM] * count,
        out_specs=jax.tree.map(lambda _: VMEM, outs),
        compiler_params=pltpu.CompilerParams(vmem_limit_bytes=megabytes << 20),
        name=name,
    )


def local(tokens, expert_ids, copy_choice, gate_weights, w_gate, w_up, w_down):
    members = lax.axis_size("expert")
    experts = members // 2
    tok_rows, chosen = expert_ids.shape
    features = tokens.shape[1]
    capacity = max(2, tok_rows * chosen // (2 * experts))
    rows = 2 * capacity
    gates = gate_weights.T
    block = jax.ShapeDtypeStruct((rows, features), jnp.bfloat16)
    target, load, *packed = call(
        functools.partial(pack_kernel, experts, capacity),
        [
            jax.ShapeDtypeStruct((chosen, tok_rows), jnp.int32),
            jax.ShapeDtypeStruct((max(8, experts), 128), jnp.float32),
        ]
        + [block] * experts,
        4,
        "pack",
        8,
    )(expert_ids.T, copy_choice.T, gates, tokens)

    def serve(mine, other):
        count = mine.shape[0]
        part, send = call(
            expert_kernel,
            [
                jax.ShapeDtypeStruct((count, features), jnp.float32),
                jax.ShapeDtypeStruct((count, features), jnp.bfloat16),
            ],
            5,
            "experts",
            20,
        )(mine, other, w_gate, w_up, w_down)
        return call(merge_kernel, jax.ShapeDtypeStruct((count, features), jnp.bfloat16), 2, "merge", 4)(
            part, swap(send, "expert", 1)
        )

    def tree(value, axis):
        mask = 1
        while mask < lax.axis_size(axis):
            value = value + swap(value, axis, mask)
            mask *= 2
        return value

    arrived = [shift(packed[step], step) for step in range(1, experts)]
    arrived = arrived[0] if experts == 2 else jnp.concatenate(arrived, axis=0)
    far = serve(arrived, swap(arrived, "expert", 1))
    near = serve(packed[0], swap(packed[0], "expert", 1))
    load_sum = tree(tree(load, "expert"), "dp")
    expert_load = load_sum[:experts, 0] / (tok_rows * lax.axis_size("dp") * members)
    returned = [shift(far[(step - 1) * rows : step * rows], -step) for step in range(1, experts)]
    combined = call(
        combine_kernel, jax.ShapeDtypeStruct((tok_rows, features), jnp.bfloat16), 2 + experts, "combine", 8
    )(target, gates, near, *returned)
    return (combined, expert_load)


def solution(mesh):
    return jax.shard_map(
        local,
        mesh=mesh,
        in_specs=(
            P(("dp", "expert"), None),
            P(("dp", "expert"), None),
            P(("dp", "expert"), None),
            P(("dp", "expert"), None),
            P(None, "expert"),
            P(None, "expert"),
            P("expert", None),
        ),
        out_specs=(P(("dp", "expert"), None), P()),
        check_vma=False,
    )
```

```python
import functools

import jax
import jax.numpy as jnp
from jax import lax
from jax.experimental import pallas as pl
from jax.experimental.pallas import tpu as pltpu
from jax.sharding import PartitionSpec as P


VMEM = pl.BlockSpec(memory_space=pltpu.VMEM)
HBM = pl.BlockSpec(memory_space=pltpu.HBM)


def swap(value, axis, mask):
    pairs = [(source, source ^ mask) for source in range(lax.axis_size(axis))]
    return lax.ppermute(value, axis, pairs)


def shift(value, step):
    members = lax.axis_size("expert")
    pairs = [(source, (source + 2 * step) % members) for source in range(members)]
    return lax.ppermute(value, "expert", pairs)


def route_kernel(
    experts, capacity, tokens_hbm, ids_hbm, copy_hbm, gate_hbm,
    tokens_ref, gate_ref, target_ref, load_ref, ids_ref, copy_ref, sems,
):
    chosen, tok_rows = ids_ref.shape
    sections = 2 * experts
    own = lax.axis_index("expert") // 2
    pairs = [(ids_hbm, ids_ref), (copy_hbm, copy_ref), (gate_hbm, gate_ref)]
    piece = tok_rows // 4 if tok_rows % 64 == 0 else tok_rows
    for start in range(0, tok_rows, piece):
        span = pl.ds(start, piece)
        pairs.append((tokens_hbm.at[span], tokens_ref.at[span]))
    copies = [pltpu.make_async_copy(src, dst, sems.at[i]) for i, (src, dst) in enumerate(pairs)]
    for copy in copies:
        copy.start()
    for copy in copies[:3]:
        copy.wait()
    section = lax.broadcasted_iota(jnp.int32, (max(16, sections), tok_rows), 0)
    keys, hots = [], []
    for k in range(chosen):
        relative = ids_ref[k : k + 1, :] - own
        relative = jnp.where(relative < 0, relative + experts, relative)
        keys.append(relative * 2 + copy_ref[k : k + 1, :])
        hots.append(jnp.where(section == keys[k], 1.0, 0.0))
    total = functools.reduce(lambda a, b: a + b, hots)
    earlier = lax.broadcasted_iota(jnp.int32, (tok_rows, tok_rows), 0) < lax.broadcasted_iota(
        jnp.int32, (tok_rows, tok_rows), 1
    )
    before = jnp.dot(
        total.astype(jnp.bfloat16),
        jnp.where(earlier, 1.0, 0.0).astype(jnp.bfloat16),
        preferred_element_type=jnp.float32,
    )
    kepts = []
    for k in range(chosen):
        rank = jnp.sum(before * hots[k], axis=0, keepdims=True).astype(jnp.int32)
        before = before + hots[k]
        retained = rank < capacity
        target_ref[k : k + 1, :] = jnp.where(retained, keys[k] * capacity + rank, -1)
        kepts.append(jnp.where(retained, gate_ref[k : k + 1, :], 0.0))
    lane = lax.broadcasted_iota(jnp.int32, load_ref.shape[1:], 1)
    load = jnp.zeros(load_ref.shape[1:], jnp.float32)
    for expert in range(experts):
        served = jnp.zeros((1, tok_rows), jnp.float32)
        for k in range(chosen):
            served = served + jnp.where(ids_ref[k : k + 1, :] == expert, kepts[k], 0.0)
        load = jnp.where(lane == expert, jnp.sum(served, axis=1, keepdims=True), load)
    first = lax.broadcasted_iota(jnp.int32, load.shape, 0) == 0
    load_ref[...] = jnp.broadcast_to(jnp.where(first, load, 0.0)[None], load_ref.shape)
    for copy in copies[3:]:
        copy.wait()


def route(experts, capacity, devices, tokens, ids, copies, gates):
    arrays = (tokens, ids, copies, gates)
    return pl.pallas_call(
        functools.partial(route_kernel, experts, capacity),
        out_shape=[
            jax.ShapeDtypeStruct(tokens.shape, tokens.dtype),
            jax.ShapeDtypeStruct(gates.shape, gates.dtype),
            jax.ShapeDtypeStruct(ids.shape, jnp.int32),
            jax.ShapeDtypeStruct((devices, 8, 128), jnp.float32),
        ],
        in_specs=[HBM] * 4,
        out_specs=[VMEM] * 4,
        scratch_shapes=[
            pltpu.VMEM(ids.shape, jnp.int32),
            pltpu.VMEM(ids.shape, jnp.int32),
            pltpu.SemaphoreType.DMA((7,)),
        ],
        compiler_params=pltpu.CompilerParams(vmem_limit_bytes=8 << 20),
        name="route",
    )(*[pltpu.with_memory_space_constraint(array, pltpu.HBM) for array in arrays])


def pack_kernel(first, rows, target_ref, tokens_ref, *packed_refs):
    chosen, tok_rows = target_ref.shape
    pieces = tokens_ref.shape[1] // packed_refs[0].shape[1]
    width = packed_refs[0].shape[1]
    for step in range(len(packed_refs) // pieces):
        place = first + step * rows + lax.broadcasted_iota(jnp.int32, (rows, tok_rows), 0)
        match = functools.reduce(
            lambda a, b: a | b, [place == target_ref[k : k + 1, :] for k in range(chosen)]
        )
        dispatch = jnp.where(match, 1.0, 0.0).astype(jnp.bfloat16)
        for piece in range(pieces):
            tokens = tokens_ref[:, piece * width : (piece + 1) * width]
            packed = jnp.dot(dispatch, tokens, preferred_element_type=jnp.float32)
            packed_refs[step * pieces + piece][...] = packed.astype(jnp.bfloat16)


def open_kernel(mine_ref, other_ref, gate_ref, up_ref, gate_out_ref, up_out_ref):
    both = jnp.concatenate([mine_ref[...], other_ref[...]], axis=0)
    width = both.shape[1]
    gate_out_ref[...] = jnp.dot(both, gate_ref[:width], preferred_element_type=jnp.float32)
    up_out_ref[...] = jnp.dot(both, up_ref[:width], preferred_element_type=jnp.float32)


def middle_kernel(
    gate_in_ref, up_in_ref, mine_ref, other_ref, gate_ref, up_ref, down_ref, hidden_ref, part_ref, send_ref
):
    both = jnp.concatenate([mine_ref[...], other_ref[...]], axis=0)
    width = both.shape[1]
    gate_act = gate_in_ref[...] + jnp.dot(both, gate_ref[width:], preferred_element_type=jnp.float32)
    up_act = up_in_ref[...] + jnp.dot(both, up_ref[width:], preferred_element_type=jnp.float32)
    hidden = (gate_act / (1.0 + jnp.exp(-gate_act)) * up_act).astype(jnp.bfloat16)
    hidden_ref[...] = hidden
    close_rows(hidden, down_ref[:, :width], part_ref, send_ref)


def close_kernel(hidden_ref, down_ref, part_ref, send_ref):
    width = part_ref.shape[1]
    close_rows(hidden_ref[...], down_ref[:, width:], part_ref, send_ref)


def close_rows(hidden, down, part_ref, send_ref):
    count = part_ref.shape[0]
    out = jnp.dot(hidden, down, preferred_element_type=jnp.float32)
    part_ref[...] = out[:count]
    send_ref[...] = out[count:].astype(jnp.bfloat16)


def expert_kernel(mine_ref, other_ref, gate_ref, up_ref, down_ref, part_ref, send_ref):
    count = mine_ref.shape[0]
    both = jnp.concatenate([mine_ref[...], other_ref[...]], axis=0)
    gate_act = jnp.dot(both, gate_ref[...], preferred_element_type=jnp.float32)
    up_act = jnp.dot(both, up_ref[...], preferred_element_type=jnp.float32)
    hidden = (gate_act / (1.0 + jnp.exp(-gate_act)) * up_act).astype(jnp.bfloat16)
    out = jnp.dot(hidden, down_ref[...], preferred_element_type=jnp.float32)
    part_ref[...] = out[:count]
    send_ref[...] = out[count:].astype(jnp.bfloat16)


def merge_kernel(part_ref, other_ref, out_ref):
    out_ref[...] = (part_ref[...] + other_ref[...].astype(jnp.float32)).astype(jnp.bfloat16)


def combine_kernel(share, target_ref, gate_ref, load_ref, near_ref, *refs):
    back_refs, (out_ref, total_ref, held_ref, sum_ref, sems) = refs[:-5], refs[-5:]
    chosen, tok_rows = target_ref.shape
    sum_ref[...] = jnp.sum(load_ref[...], axis=0)[:1, : sum_ref.shape[1]] / share
    copies = [pltpu.make_async_copy(sum_ref, total_ref, sems.at[0])]
    copies[0].start()
    half = back_refs[0].shape[1]
    blocks = len(back_refs) // 2
    slots = near_ref.shape[0] + blocks * back_refs[0].shape[0]
    slot = lax.broadcasted_iota(jnp.int32, (tok_rows, slots), 1)
    selects, scales = [], []
    for k in range(chosen):
        column = jnp.broadcast_to(target_ref[k : k + 1, :], (slots, tok_rows)).T
        selects.append(jnp.where(column == slot, 1.0, 0.0).astype(jnp.bfloat16))
        scales.append(jnp.broadcast_to(gate_ref[k : k + 1, :], (128, tok_rows)).T[:, :1])
    count = sems.shape[0] - 1
    width = 2 * half // count
    for i in range(count):
        piece, start = divmod(i * width, half)
        wide = pl.ds(i * width, width)
        backs = [ref[:, start : start + width] for ref in back_refs[piece * blocks : (piece + 1) * blocks]]
        results = jnp.concatenate([near_ref[:, wide]] + backs, axis=0)
        combined = None
        for k in range(chosen):
            term = scales[k] * jnp.dot(selects[k], results, preferred_element_type=jnp.float32)
            combined = term if combined is None else combined + term
        held_ref[:, wide] = combined.astype(jnp.bfloat16)
        copies.append(pltpu.make_async_copy(held_ref.at[:, wide], out_ref.at[:, wide], sems.at[i + 1]))
        copies[-1].start()
    for copy in copies:
        copy.wait()


def combine(share, experts, target, gates, load, near, backs):
    tok_rows = target.shape[1]
    features = near.shape[1]
    count = 4 if features % 512 == 0 else 2
    out, total = pl.pallas_call(
        functools.partial(combine_kernel, share),
        out_shape=[
            jax.ShapeDtypeStruct((tok_rows, features), jnp.bfloat16),
            jax.ShapeDtypeStruct((1, experts), jnp.float32),
        ],
        in_specs=[VMEM] * (4 + len(backs)),
        out_specs=[HBM, HBM],
        scratch_shapes=[
            pltpu.VMEM((tok_rows, features), jnp.bfloat16),
            pltpu.VMEM((1, experts), jnp.float32),
            pltpu.SemaphoreType.DMA((count + 1,)),
        ],
        compiler_params=pltpu.CompilerParams(vmem_limit_bytes=8 << 20),
        name="combine",
    )(target, gates, load, near, *backs)
    return out, total[0]


def call(kernel, outs, count, megabytes, cost=None):
    return pl.pallas_call(
        kernel,
        out_shape=outs,
        in_specs=[VMEM] * count,
        out_specs=jax.tree.map(lambda _: VMEM, outs),
        compiler_params=pltpu.CompilerParams(vmem_limit_bytes=megabytes << 20),
        cost_estimate=cost,
    )


def local(tokens, expert_ids, copy_choice, gate_weights, w_gate, w_up, w_down):
    members = lax.axis_size("expert")
    experts = members // 2
    tok_rows, chosen = expert_ids.shape
    features = tokens.shape[1]
    capacity = max(2, tok_rows * chosen // (2 * experts))
    rows = 2 * capacity
    half = features // 2
    devices = lax.axis_size("dp") * members
    tokens, gates, target, load = route(
        experts, capacity, devices, tokens, expert_ids.T, copy_choice.T, gate_weights.T
    )
    packed = call(
        functools.partial(pack_kernel, rows, rows),
        [jax.ShapeDtypeStruct((rows, half), jnp.bfloat16)] * (2 * (experts - 1)),
        2,
        8,
        pl.CostEstimate(flops=30_000_000_000, transcendentals=0, bytes_accessed=0),
    )(target, tokens)
    arrived = []
    for piece in range(2):
        blocks = [shift(packed[2 * (step - 1) + piece], step) for step in range(1, experts)]
        arrived.append(blocks[0] if experts == 2 else jnp.concatenate(blocks, axis=0))
    (packed_near,) = call(
        functools.partial(pack_kernel, 0, rows),
        [jax.ShapeDtypeStruct((rows, features), jnp.bfloat16)],
        2,
        8,
    )(target, tokens)

    def serve(mine):
        count = mine.shape[0]
        other = swap(mine, "expert", 1)
        part, send = call(
            expert_kernel,
            [
                jax.ShapeDtypeStruct((count, features), jnp.float32),
                jax.ShapeDtypeStruct((count, features), jnp.bfloat16),
            ],
            5,
            20,
        )(mine, other, w_gate, w_up, w_down)
        other = swap(send, "expert", 1)
        return call(
            merge_kernel, jax.ShapeDtypeStruct((count, features), jnp.bfloat16), 2, 4
        )(part, other)

    load = lax.all_to_all(load, ("dp", "expert"), 0, 0, tiled=True)

    near = serve(packed_near)
    count = (experts - 1) * rows
    acts = jax.ShapeDtypeStruct((2 * count, w_gate.shape[1]), jnp.float32)
    part = jax.ShapeDtypeStruct((count, half), jnp.float32)
    send = jax.ShapeDtypeStruct((count, half), jnp.bfloat16)
    others = []
    for piece in range(2):
        others.append(swap(arrived[piece], "expert", 1))
    gate_act, up_act = call(open_kernel, [acts, acts], 4, 20)(arrived[0], others[0], w_gate, w_up)
    parts, sends = [None, None], [None, None]
    hidden, parts[0], sends[0] = call(
        middle_kernel,
        [jax.ShapeDtypeStruct((2 * count, w_gate.shape[1]), jnp.bfloat16), part, send],
        7,
        20,
    )(gate_act, up_act, arrived[1], others[1], w_gate, w_up, w_down)
    parts[1], sends[1] = call(close_kernel, [part, send], 2, 20)(hidden, w_down)
    returned = []
    for piece in range(2):
        other = swap(sends[piece], "expert", 1)
        far = call(merge_kernel, send, 2, 4)(parts[piece], other)
        returned += [shift(far[(step - 1) * rows : step * rows], -step) for step in range(1, experts)]
    return combine(tok_rows * devices, experts, target, gates, load, near, returned)


def solution(mesh):
    return jax.shard_map(
        local,
        mesh=mesh,
        in_specs=(
            P(("dp", "expert"), None),
            P(("dp", "expert"), None),
            P(("dp", "expert"), None),
            P(("dp", "expert"), None),
            P(None, "expert"),
            P(None, "expert"),
            P("expert", None),
        ),
        out_specs=(P(("dp", "expert"), None), P()),
        check_vma=False,
    )
```
